32 devices in a mesh: tok: 4 (over z), hid: 8 (over y, x, core).
Axes of the slice: x: 2, y: 2, z: 4, core: 2. Of those that a mesh axis runs over, the one named last changes fastest.
Arguments:
- tokens: bfloat16 [4096, 8192], P('tok', 'hid'), may hold values from -6 to 6
- qkv_weight: bfloat16 [8192, 10240], P('tok', 'hid'), may hold values from -0.09375 to 0.09375
- qkv_cotangent: bfloat16 [4096, 10240], P('tok', 'hid'), may hold values from -6 to 6
Outputs:
- projected: bfloat16 [4096, 10240], P('tok', 'hid')
- input_grad: bfloat16 [4096, 8192], P('tok', 'hid')
- weight_grad: bfloat16 [8192, 10240], P('tok', 'hid')
The draws below stay inside these ranges and needn't reach their ends.
All inputs are finite; a program needn't handle non-finite values.
Results may differ from the reference program's by a relative error of at most 0.012.
Values may be sent and summed in bfloat16 or wider, within the bound.
A program may use at most 192 MiB of HBM per device.

```python
import jax
import jax.numpy as jnp
from jax import lax

D = 8192
QKV = 10240
TOKENS = 4096
N_HID = 8


def raised(result, own_key, source, target, blocks, factor):
    owner, partner = [(jnp.arange(result.shape[dim]) // (result.shape[dim] // blocks)).reshape([-1 if axis == dim else 1 for axis in range(result.ndim)]) for dim in (source, target)]
    chosen = jax.random.permutation(own_key, blocks)[partner]
    strong = (owner == chosen) | (owner == (partner + blocks // 2) % blocks)
    return jnp.where(strong, factor * result, result)


def block_levels(key, shape, pieces, low, top_value):
    level, own = 1.0, jax.random.fold_in(key, 6)
    for axis_at, blocks in pieces:
        draws = jnp.exp(jax.random.uniform(jax.random.fold_in(own, axis_at), (blocks,), jnp.float32, low / len(pieces), top_value / len(pieces)))
        level = level * jnp.repeat(draws, shape[axis_at] // blocks).reshape([-1 if axis == axis_at else 1 for axis in range(len(shape))])
    return level


def gaussian(stream_key, extent, scale, limit, split=(), kind=jnp.bfloat16):
    level = block_levels(stream_key, extent, split, -0.22, 0.18) if split else 1.0
    array = jax.random.normal(stream_key, extent, jnp.float32) * scale * level
    return jnp.minimum(jnp.maximum(array, -limit), limit).astype(kind)


def noise_with(rng, shape, width, reach, split, heavy, dtype=jnp.bfloat16):
    result = width * jax.random.normal(rng, shape, jnp.float32)
    if split:
        result = result * block_levels(rng, shape, split, -0.22, 0.18)
    return jnp.clip(raised(result, jax.random.fold_in(rng, 3), *heavy), -reach, reach).astype(dtype)


def setup_inputs(seed: int = 0) -> dict:
    key_of = jax.random.split(jax.random.key(seed), 4)
    tokens = noise_with(key_of[0], (TOKENS, D), 1.0, 6.0, ((0, 4), (1, 8)), (0, 1, 8, 2.0))
    qkv_weight = noise_with(key_of[1], (D, QKV), D ** -0.5, 0.09375, ((0, 4), (1, 8)), (1, 0, 8, 2.0))
    qkv_cotangent = gaussian(key_of[2], (TOKENS, QKV), 1.0, 6.0, ((0, 4), (1, 8)))
    return {"tokens": tokens, "qkv_weight": qkv_weight, "qkv_cotangent": qkv_cotangent}


def reference(tokens, qkv_weight, qkv_cotangent):
    hp = lax.Precision.HIGHEST
    tok32 = tokens.astype(jnp.float32)
    wgt32 = qkv_weight.astype(jnp.float32)
    cot32 = qkv_cotangent.astype(jnp.float32)
    projected = jnp.dot(tok32, wgt32, precision=hp).astype(jnp.bfloat16)
    group_width = QKV // N_HID
    summed = jnp.zeros((TOKENS, D), jnp.float32)
    for group in range(N_HID):
        lower = group * group_width
        partial_sum = jnp.dot(cot32[:, lower:lower + group_width], wgt32[:, lower:lower + group_width].T, precision=hp)
        partial_sum = lax.optimization_barrier(partial_sum.astype(jnp.bfloat16))
        summed = summed + partial_sum.astype(jnp.float32)
    input_grad = summed.astype(jnp.bfloat16)
    weight_grad = (jnp.dot(tok32.T, cot32, precision=hp) * (TOKENS ** -0.5)).astype(jnp.bfloat16)
    return (projected, input_grad, weight_grad)
```

```python
import jax
import jax.numpy as jnp
from jax import lax
from jax.sharding import PartitionSpec as P


F32, BF16 = jnp.float32, jnp.bfloat16


def group_sum(block, weight):
    return lax.dot_general(
        block, weight, (((1,), (1,)), ((), ())), preferred_element_type=F32
    ).astype(BF16)


def local(tokens, qkv_weight, qkv_cotangent):
    n_tok, n_hid = lax.axis_size("tok"), lax.axis_size("hid")
    me = lax.axis_index("tok")
    rows, wide = tokens.shape[0], qkv_weight.shape[0]
    right = [(i, i + 1) for i in range(n_tok - 1)]
    left = [(i + 1, i) for i in range(n_tok - 1)]

    split = lax.all_to_all(tokens, "hid", split_axis=0, concat_axis=1, tiled=True)
    split = split.reshape(split.shape[0], n_tok, wide).transpose(1, 0, 2)
    split = lax.all_to_all(split, "tok", split_axis=0, concat_axis=0)
    from_low, from_high = [qkv_cotangent], [qkv_cotangent]
    for step in range(n_tok - 1):
        if step == 1:
            split, from_low[1], from_high[1] = lax.optimization_barrier(
                (split, from_low[1], from_high[1])
            )
        from_low.append(lax.ppermute(from_low[-1], "tok", right))
        from_high.append(lax.ppermute(from_high[-1], "tok", left))

    first = lax.psum_scatter(
        group_sum(qkv_cotangent, qkv_weight), "hid", scatter_dimension=0, tiled=True
    )
    split, first = lax.optimization_barrier((split, first))
    features = lax.all_gather(split, "hid", axis=1, tiled=True)

    both = jnp.minimum(me, n_tok - 1 - me)
    slots, owners = [qkv_cotangent], [me]
    for s in range(1, n_tok):
        near = s <= 2 * both
        distance = jnp.where(near, (s + 1) // 2, s - both)
        low = jnp.where(near, s % 2 == 1, me > n_tok - 1 - me)
        block = jnp.zeros_like(qkv_cotangent)
        for d in range(1, s + 1):
            block = jnp.where(
                distance == d, jnp.where(low, from_low[d], from_high[d]), block
            )
        slots.append(block)
        owners.append(jnp.where(low, me - distance, me + distance))

    grads = jnp.zeros((n_tok, rows // n_hid, wide), BF16)
    grads = lax.dynamic_update_index_in_dim(grads, first, me, 0)
    for s in range(1, n_tok):
        backward = group_sum(slots[s], qkv_weight)
        if s == 1:
            backward, features = lax.optimization_barrier((backward, features))
        piece = lax.psum_scatter(backward, "hid", scatter_dimension=0, tiled=True)
        grads = lax.dynamic_update_index_in_dim(grads, piece, owners[s], 0)
    grads = lax.all_to_all(grads, "tok", split_axis=0, concat_axis=0)
    grads = grads.transpose(1, 0, 2).reshape(rows // n_hid, n_tok * wide)
    input_grad = lax.all_to_all(grads, "hid", split_axis=1, concat_axis=0, tiled=True)

    partial = jnp.dot(
        features.reshape(n_tok * rows, wide), qkv_weight, preferred_element_type=F32
    ).reshape(n_tok, rows, qkv_weight.shape[1])

    def own(index):
        return lax.dynamic_index_in_dim(partial, jnp.clip(index, 0, n_tok - 1), 0, False)

    low_sum = high_sum = None
    for s in range(1, n_tok):
        hop = n_tok - s
        up, down = own(me + hop), own(me - hop)
        if low_sum is not None:
            up, down = up + low_sum.astype(F32), down + high_sum.astype(F32)
        low_sum = lax.ppermute(up.astype(BF16), "tok", right[:s])
        high_sum = lax.ppermute(down.astype(BF16), "tok", left[n_tok - 1 - s:])
    total = own(me)
    if low_sum is not None:
        total = total + low_sum.astype(F32) + high_sum.astype(F32)
    projected = total.astype(BF16)

    blocks = jnp.zeros((n_tok,) + qkv_cotangent.shape, BF16)
    for block, owner in zip(slots, owners):
        blocks = lax.dynamic_update_index_in_dim(blocks, block, owner, 0)
    weight_sum = lax.dot_general(
        features.reshape(n_tok * rows, wide), blocks.reshape(n_tok * rows, -1),
        (((0,), (0,)), ((), ())), preferred_element_type=F32,
    )
    weight_grad = (weight_sum * float(rows * n_tok) ** (-0.5)).astype(BF16)
    return projected, input_grad, weight_grad


def solution(mesh):
    specs = (P("tok", "hid"),) * 3
    return jax.shard_map(local, mesh=mesh, in_specs=specs, out_specs=specs, check_vma=False)
```
